1024 devices in a mesh: ctx: 32 (over z_lo, core), mp: 32 (over y, x, z_hi).
Axes of the slice: x: 4, y: 4, z: 32 (z_hi: 2, z_lo: 16; z = z_hi * 16 + z_lo), core: 2. Of those that a mesh axis runs over, the one named last changes fastest.
Arguments:
- grad_out: bfloat16 [16384, 4096], P('ctx', 'mp'), may hold values from -6 to 6
- proj_out: bfloat16 [4096, 4096], P('mp', 'ctx'), may hold values from -0.09375 to 0.09375
- query: bfloat16 [16384, 4096], P('ctx', 'mp'), may hold values from -6 to 6
- key_in: bfloat16 [16384, 4096], P('ctx', 'mp'), may hold values from -6 to 6
- value_in: bfloat16 [16384, 4096], P('ctx', 'mp'), may hold values from -6 to 6
- filters: float32 [4096, 16384], P(('mp', 'ctx')), may hold values from -0.046875 to 0.046875
Outputs:
- grad_query: bfloat16 [16384, 4096], P('ctx', 'mp')
- grad_key: bfloat16 [16384, 4096], P('ctx', 'mp')
- grad_value: bfloat16 [16384, 4096], P('ctx', 'mp')
- filter_grad: float32 [4096, 16384], P(('mp', 'ctx'))
The draws below stay inside these ranges and needn't reach their ends.
All inputs are finite; a program needn't handle non-finite values.
Results may differ from the reference program's by a relative error of at most 0.013.
Values may be sent and summed in bfloat16 or wider, within the bound.
A program may use at most 64 MiB of HBM per device.

```python
import math
import jax
import jax.numpy as jnp
from jax import lax

D = 4096
SEQ = 16384


def block_levels(stream_key, dims, cuts, smallest, largest):
    factor_of, own = 1.0, jax.random.fold_in(stream_key, 6)
    for dim, shards_of in cuts:
        heights = jnp.exp(jax.random.uniform(jax.random.fold_in(own, dim), (shards_of,), jnp.float32, smallest / len(cuts), largest / len(cuts)))
        factor_of = factor_of * jnp.repeat(heights, dims[dim] // shards_of).reshape([-1 if axis == dim else 1 for axis in range(len(dims))])
    return factor_of


def normal_values(key, dims, deviation, most, pieces=(), kind=jnp.bfloat16):
    factor_of = block_levels(key, dims, pieces, -0.22, 0.18) if pieces else 1.0
    drawn = jax.random.normal(key, dims, jnp.float32) * deviation * factor_of
    return jnp.minimum(jnp.maximum(drawn, -most), most).astype(kind)


def setup_inputs(seed: int = 0) -> dict:
    key_list = jax.random.split(jax.random.key(seed), 7)
    return {
        "grad_out": normal_values(key_list[0], (SEQ, D), 1.0, 6.0, ((0, 32), (1, 32))),
        "proj_out": normal_values(key_list[1], (D, D), D ** -0.5, 0.09375, ((0, 32), (1, 32))),
        "query": normal_values(key_list[2], (SEQ, D), 1.0, 6.0, ((0, 32), (1, 32))),
        "key_in": normal_values(key_list[3], (SEQ, D), 1.0, 6.0, ((0, 32), (1, 32))),
        "value_in": normal_values(key_list[4], (SEQ, D), 1.0, 6.0, ((0, 32), (1, 32))),
        "filters": normal_values(key_list[5], (D, SEQ), SEQ ** -0.5, 0.046875, ((0, 1024),), jnp.float32),
    }


def channel_block(blocks):
    gated, scaled, kernel = blocks
    length_all = 2 * SEQ
    gated_spec = jnp.fft.rfft(gated, n=length_all, axis=1)
    scaled_spec = jnp.fft.rfft(scaled, n=length_all, axis=1)
    kernel_spec = jnp.fft.rfft(kernel, n=length_all, axis=1)
    conv_out = jnp.fft.irfft(kernel_spec * gated_spec, n=length_all, axis=1)[:, :SEQ]
    grad_gated = jnp.fft.irfft(scaled_spec * jnp.conj(kernel_spec), n=length_all, axis=1)[:, :SEQ]
    grad_kernel = jnp.fft.irfft(scaled_spec * jnp.conj(gated_spec), n=length_all, axis=1)[:, :SEQ]
    return (conv_out, grad_gated, grad_kernel)

def reference(grad_out, proj_out, query, key_in, value_in, filters):
    grad_mix = jnp.dot(grad_out, proj_out.T, preferred_element_type=jnp.float32).astype(jnp.bfloat16)
    gated = (key_in.astype(jnp.float32) * value_in.astype(jnp.float32)).astype(jnp.bfloat16)
    scaled = (grad_mix.astype(jnp.float32) * query.astype(jnp.float32)).astype(jnp.bfloat16)
    width_block = min(256, D)

    def to_blocks(values):
        return values.astype(jnp.float32).T.reshape(D // width_block, width_block, SEQ)
    kernels = filters.astype(jnp.float32).reshape(D // width_block, width_block, SEQ)
    conv_out, grad_gated, grad_kernel = lax.map(channel_block, (to_blocks(gated), to_blocks(scaled), kernels))
    conv_out = conv_out.reshape(D, SEQ).T.astype(jnp.bfloat16)
    grad_gated = grad_gated.reshape(D, SEQ).T.astype(jnp.bfloat16)
    filter_grad = (grad_kernel.reshape(D, SEQ) / math.sqrt(SEQ)).astype(jnp.float32)
    grad_query = (grad_mix.astype(jnp.float32) * conv_out.astype(jnp.float32)).astype(jnp.bfloat16)
    grad_key = (grad_gated.astype(jnp.float32) * value_in.astype(jnp.float32)).astype(jnp.bfloat16)
    grad_value = (grad_gated.astype(jnp.float32) * key_in.astype(jnp.float32)).astype(jnp.bfloat16)
    return (grad_query, grad_key, grad_value, filter_grad)
```

```python
import math

import jax
import jax.numpy as jnp
import ml_dtypes
import numpy as np
from jax import lax
from jax.experimental import pallas as pl
from jax.experimental.pallas import tpu as pltpu
from jax.sharding import Mesh
from jax.sharding import PartitionSpec as P

MESH = pl.DeviceIdType.MESH
CTX = ("zl", "core")
MP = ("y", "x", "zh")
EVERY = ("y", "x", "zh", "zl", "core")

BF = jnp.bfloat16
F32 = jnp.float32


def split_table(table):
    high = table.astype(np.float32).astype(ml_dtypes.bfloat16)
    low = (table - high.astype(np.float64)).astype(np.float32).astype(ml_dtypes.bfloat16)
    return (high, low)


def make_tables():
    size = 128
    order = np.arange(size).reshape(32, 4).T.reshape(-1)
    freq = np.arange(size) + 0.25
    angle_first = 2.0 * math.pi * np.outer(freq, order) / size
    first = np.concatenate([np.cos(angle_first), -np.sin(angle_first)], axis=0)
    angle_twist = 2.0 * math.pi * np.outer(freq, np.arange(size)) / (size * size)
    twist_re, twist_im = (np.cos(angle_twist), -np.sin(angle_twist))
    angle_second = 2.0 * math.pi * (np.outer(np.arange(size), np.arange(size)) % size) / size
    cos, sin = (np.cos(angle_second), np.sin(angle_second))
    second = np.block([[cos, -sin], [sin, cos]])
    second_back = np.block([[cos, sin], [-sin, cos]])
    first_back = np.concatenate([np.cos(angle_first).T, -np.sin(angle_first).T], axis=1) / (size * size)
    return (
        *split_table(first),
        twist_re.astype(np.float32),
        twist_im.astype(np.float32),
        *split_table(second),
        *split_table(second_back),
        *split_table(first_back),
    )


def dot(left, right):
    return lax.dot_general(left, right, (((1,), (0,)), ((), ())), preferred_element_type=F32)


def halves(values):
    high = values.astype(BF)
    return (high, (values - high.astype(F32)).astype(BF))


def table_dot(table, values, exact=False):
    if exact:
        high = values.astype(BF)
        return dot(table[0], high) + dot(table[1], high)
    high, low = halves(values)
    return dot(table[0], high) + (dot(table[1], high) + dot(table[0], low))


def dot_table(values, table):
    high, low = halves(values)
    return dot(high, table[0]) + (dot(high, table[1]) + dot(low, table[0]))


def forward(signals, first, twist, second, exact):
    spread = table_dot(first, jnp.concatenate(signals, axis=1), exact)
    rows = []
    for ch in range(4):
        re = spread[0:128, ch * 128 : ch * 128 + 128]
        im = spread[128:256, ch * 128 : ch * 128 + 128]
        turned = [re * twist[0] - im * twist[1], re * twist[1] + im * twist[0]]
        rows.append(jnp.concatenate(turned, axis=1))
    return dot_table(jnp.concatenate(rows, axis=0), second)


def backward(spec_re, spec_im, first_back, twist, second_back):
    gathered = dot_table(jnp.concatenate([spec_re, spec_im], axis=1), second_back)
    upper, lower = ([], [])
    for ch in range(4):
        re = gathered[ch * 128 : ch * 128 + 128, 0:128]
        im = gathered[ch * 128 : ch * 128 + 128, 128:256]
        upper.append(re * twist[0] + im * twist[1])
        lower.append(im * twist[0] - re * twist[1])
    stacked = jnp.concatenate([jnp.concatenate(upper, axis=1), jnp.concatenate(lower, axis=1)], axis=0)
    return table_dot(first_back, stacked)


def kernel(
    g, w, q, k, v, f, f1h, f1l, tre, tim, s2h, s2l, b2h, b2l, i1h, i1l,
    gm_o, conv_o, gg_o, fg_o,
    gbuf, wbuf, relay, sbuf, rbuf, rows, acc, fspec, gspec,
    loc_sem, z_send, z_recv, p_send, p_recv, w_send, w_recv, c_send, c_recv, a_send, a_recv,
):
    zl, core = (lax.axis_index("zl"), lax.axis_index("core"))
    y, x, zh = (lax.axis_index("y"), lax.axis_index("x"), lax.axis_index("zh"))
    me = zl * 2 + core
    x_up, x_dn, x_far = ((x + 1) % 4, (x + 3) % 4, (x + 2) % 4)
    y_up, y_dn, y_far = ((y + 1) % 4, (y + 3) % 4, (y + 2) % 4)
    z = zh * 16 + zl
    z_up, z_dn = ((z + 8) % 32, (z + 24) % 32)
    dev_up = {"zl": z_up % 16, "zh": z_up // 16}
    dev_dn = {"zl": z_dn % 16, "zh": z_dn // 16}
    other = 1 - zh

    def remote(src, dst, send, recv, dev):
        return pltpu.make_async_remote_copy(
            src_ref=src, dst_ref=dst, send_sem=send, recv_sem=recv, device_id=dev, device_id_type=MESH
        )

    barrier = pltpu.get_barrier_semaphore()
    z_next, z_prev = ((z + 1) % 32, (z + 31) % 32)
    dev_next = {"zl": z_next % 16, "zh": z_next // 16}
    dev_prev = {"zl": z_prev % 16, "zh": z_prev // 16}
    for dev in (
        {"x": x_up}, {"x": x_dn}, {"y": y_up}, {"y": y_dn}, dev_up, dev_dn, {"core": 1 - core}, dev_next, dev_prev
    ):
        pl.semaphore_signal(barrier, inc=1, device_id=dev, device_id_type=MESH)

    own_g = pltpu.make_async_copy(g, gbuf.at[zh, y, x], loc_sem.at[0])
    own_w = pltpu.make_async_copy(w, wbuf.at[core, zl], loc_sem.at[1])
    own_g.start()
    own_w.start()
    own_g.wait()
    own_w.wait()
    pl.semaphore_wait(barrier, 9)

    pending = []

    leg_up = remote(g.at[0:256], relay.at[0], z_send.at[0], z_recv.at[0], dev_up)
    leg_dn = remote(g.at[256:512], relay.at[1], z_send.at[1], z_recv.at[1], dev_dn)
    leg_up.start()
    leg_dn.start()
    pending += [leg_up, leg_dn]

    def second_legs():
        leg_up.wait_recv()
        leg_dn.wait_recv()
        on_up = remote(
            relay.at[0], gbuf.at[1 - z_up // 16, y, x, 0:256], z_send.at[2], z_recv.at[2], dev_up
        )
        on_dn = remote(
            relay.at[1], gbuf.at[1 - z_dn // 16, y, x, 256:512], z_send.at[3], z_recv.at[3], dev_dn
        )
        on_up.start()
        on_dn.start()
        pending.extend([on_up, on_dn])
        return (on_up, on_dn)

    def stage_pair(h, half, stage, up, dn, dev_next, dev_prev):
        copies = []
        for way, (ref, dev) in enumerate(((up, dev_next), (dn, dev_prev))):
            copies.append(
                remote(ref, ref, p_send.at[h, half, stage, way], p_recv.at[h, half, stage, way], dev)
            )
        return copies

    def plane(slot, h):
        to_x, from_x = ({"x": x_up}, {"x": x_dn})
        to_y, from_y = ({"y": y_up}, {"y": y_dn})
        low, high = (pl.ds(0, 256), pl.ds(256, 256))
        stages = (
            lambda: (
                (0, gbuf.at[slot, y, x, low], gbuf.at[slot, y, x, low], to_x, from_x),
                (1, gbuf.at[slot, y, x, high], gbuf.at[slot, y, x, high], to_y, from_y),
            ),
            lambda: (
                (0, gbuf.at[slot, y, x_dn, pl.ds(0, 128)], gbuf.at[slot, y, x_up, pl.ds(128, 128)], to_x, from_x),
                (1, gbuf.at[slot, y_dn, x, pl.ds(256, 128)], gbuf.at[slot, y_up, x, pl.ds(384, 128)], to_y, from_y),
            ),
            lambda: (
                (0, gbuf.at[slot, y, :, low], gbuf.at[slot, y, :, low], to_y, from_y),
                (1, gbuf.at[slot, :, x, high], gbuf.at[slot, :, x, high], to_x, from_x),
            ),
            lambda: (
                (0, gbuf.at[slot, y_dn, 0:2, low], gbuf.at[slot, y_up, 2:4, low], to_y, from_y),
                (1, gbuf.at[slot, 0:2, x_dn, high], gbuf.at[slot, 2:4, x_up, high], to_x, from_x),
            ),
        )
        in_flight = []
        for stage, parts in enumerate(stages):
            for copy in in_flight:
                copy.wait_recv()
            in_flight = []
            for half, up, dn, dev_next, dev_prev in parts():
                in_flight += stage_pair(h, half, stage, up, dn, dev_next, dev_prev)
            for copy in in_flight:
                copy.start()
            pending.extend(in_flight)
            yield
        for copy in in_flight:
            copy.wait_recv()
        yield

    def chain_copy(block, way, step):
        ref = wbuf.at[core, block]
        dev = {"zl": zl + 1} if way == 0 else {"zl": zl - 1}
        return remote(ref, ref, w_send.at[way, step], w_recv.at[block], dev)

    def chain(step):
        for way, block in ((0, zl - step), (1, zl + step)):
            ok = block >= 0 if way == 0 else block <= 15
            more = zl < 15 if way == 0 else zl > 0

            @pl.when(ok)
            def _():
                if step > 0:
                    chain_copy(block, way, step).wait_recv()

                @pl.when(more)
                def _():
                    chain_copy(block, way, step).start()

    def chain_sent(step):
        for way, block in ((0, zl - step), (1, zl + step)):
            ok = block >= 0 if way == 0 else block <= 15
            more = zl < 15 if way == 0 else zl > 0

            @pl.when(jnp.logical_and(ok, more))
            def _():
                chain_copy(block, way, step).wait_send()

    def slab_copy(which, peer):
        return remote(
            sbuf.at[which, peer],
            rbuf.at[which, me],
            a_send.at[which, peer],
            a_recv.at[which, me],
            {"zl": peer // 2, "core": peer % 2},
        )

    def all_to_all_start(which):
        mine = pltpu.make_async_copy(sbuf.at[which, me], rbuf.at[which, me], a_recv.at[which, me])
        mine.start()

        def body(d, carry):
            slab_copy(which, (me + d) % 32).start()
            return carry

        lax.fori_loop(1, 32, body, 0)

    def all_to_all_wait(which):
        def body(d, carry):
            src = (me + d) % 32
            remote(
                sbuf.at[which, src], rbuf.at[which, src], a_send.at[which, src], a_recv.at[which, src],
                {"zl": src // 2, "core": src % 2},
            ).wait_recv()
            return carry

        lax.fori_loop(1, 32, body, 0)
        pltpu.make_async_copy(sbuf.at[which, me], rbuf.at[which, me], a_recv.at[which, me]).wait()

    def all_to_all_sent(which):
        def body(d, carry):
            slab_copy(which, (me + d) % 32).wait_send()
            return carry

        lax.fori_loop(1, 32, body, 0)

    def to_slabs(which, values):
        for p in range(4):
            rows[pl.ds(p, 128, stride=4), :] = values[p * 128 : p * 128 + 128, :].T
        sbuf[which] = rows[...].astype(BF).reshape(32, 16, 128)

    def from_slabs(which, out):
        rows[...] = rbuf[which].astype(F32).reshape(512, 128)
        for p in range(4):
            out[p * 128 : p * 128 + 128, :] = rows[pl.ds(p, 128, stride=4), :].T.astype(BF)

    def signals(which):
        rows[...] = rbuf[which].astype(F32).reshape(512, 128)
        return [
            jnp.concatenate([rows[pl.ds(ch * 4 + p, 32, stride=16), :] for p in range(4)], axis=0)
            for ch in range(4)
        ]

    def back_slabs(which, result):
        for ch in range(4):
            for p in range(4):
                rows[pl.ds(ch * 4 + p, 32, stride=16), :] = result[
                    p * 32 : p * 32 + 32, ch * 128 : ch * 128 + 128
                ]
        sbuf[which] = rows[...].astype(BF).reshape(32, 16, 128)

    def tables():
        return (
            (f1h[...], f1l[...]),
            (tre[...], tim[...]),
            (s2h[...], s2l[...]),
            (b2h[...], b2l[...]),
            (i1h[...], i1l[...]),
        )

    def multiply(slot):
        total = None
        for yy in range(4):
            for xx in range(4):
                block = yy * 4 + xx
                part = lax.dot_general(
                    gbuf[slot, yy, xx],
                    wbuf[slot, block],
                    (((1,), (1,)), ((), ())),
                    preferred_element_type=F32,
                )
                total = part if total is None else total + part
        return total

    own = plane(zh, 0)
    next(own)
    chain(0)
    gated = (k[...].astype(F32) * v[...].astype(F32)).astype(BF).astype(F32)
    to_slabs(0, gated)
    chain(1)
    next(own)
    chain(2)
    next(own)
    for step in (3, 4, 5):
        chain(step)
    next(own)
    for step in (6, 7):
        chain(step)
    on_up, on_dn = second_legs()
    for step in range(8, 16):
        chain(step)
    swap = remote(wbuf.at[core], wbuf.at[core], c_send.at[0], c_recv.at[0], {"core": 1 - core})
    swap.start()
    pending.append(swap)
    next(own)
    swap.wait_recv()
    all_to_all_start(0)

    on_up.wait_recv()
    on_dn.wait_recv()
    rest = plane(other, 1)
    next(rest)
    first, twist, second, second_back, first_back = tables()
    filters = [
        jnp.concatenate([f[ch, pl.ds(p, 32, stride=4), :] for p in range(4)], axis=0) for ch in range(4)
    ]
    fspec[...] = forward(filters, first, twist, second, False)
    next(rest)
    next(rest)
    acc[...] = multiply(zh)
    next(rest)
    next(rest)
    mixed = (acc[...] + multiply(other)).astype(BF)
    gm_o[...] = mixed
    to_slabs(1, mixed.astype(F32) * q[...].astype(F32))
    all_to_all_start(1)

    all_to_all_wait(0)
    gspec[...] = forward(signals(0), first, twist, second, True)
    f_re, f_im = (fspec[:, 0:128], fspec[:, 128:256])
    g_re, g_im = (gspec[:, 0:128], gspec[:, 128:256])
    back_slabs(
        2, backward(f_re * g_re - f_im * g_im, f_re * g_im + f_im * g_re, first_back, twist, second_back)
    )
    all_to_all_start(2)

    all_to_all_wait(1)
    spec = forward(signals(1), first, twist, second, True)
    s_re, s_im = (spec[:, 0:128], spec[:, 128:256])
    f_re, f_im = (fspec[:, 0:128], fspec[:, 128:256])
    back_slabs(
        3, backward(s_re * f_re + s_im * f_im, s_im * f_re - s_re * f_im, first_back, twist, second_back)
    )
    all_to_all_start(3)
    g_re, g_im = (gspec[:, 0:128], gspec[:, 128:256])
    lags = backward(s_re * g_re + s_im * g_im, s_im * g_re - s_re * g_im, first_back, twist, second_back)
    for ch in range(4):
        for p in range(4):
            fg_o[ch, pl.ds(p, 32, stride=4), :] = (
                lags[p * 32 : p * 32 + 32, ch * 128 : ch * 128 + 128] * (1.0 / 128.0)
            )
    all_to_all_wait(2)
    from_slabs(2, conv_o)
    all_to_all_wait(3)
    from_slabs(3, gg_o)

    for copy in pending:
        copy.wait_send()
    for step in range(16):
        chain_sent(step)
    for which in range(4):
        all_to_all_sent(which)


def product(left, right):
    return (left.astype(F32) * right.astype(F32)).astype(BF)


def body(grad_out, proj_out, query, key_in, value_in, filters):
    tables = make_tables()
    operands = (grad_out, proj_out, query, key_in, value_in, filters.reshape(4, 128, 128), *tables)
    tile = jax.ShapeDtypeStruct((512, 128), BF)
    vmem = pl.BlockSpec(memory_space=pltpu.VMEM)
    dma = pltpu.SemaphoreType.DMA
    mixed, conv_out, grad_gated, filter_grad = pl.pallas_call(
        kernel,
        out_shape=(tile, tile, tile, jax.ShapeDtypeStruct((4, 128, 128), F32)),
        in_specs=[vmem] * len(operands),
        out_specs=(vmem,) * 4,
        scratch_shapes=[
            pltpu.VMEM((2, 4, 4, 512, 128), BF),
            pltpu.VMEM((2, 16, 128, 128), BF),
            pltpu.VMEM((2, 256, 128), BF),
            pltpu.VMEM((4, 32, 16, 128), BF),
            pltpu.VMEM((4, 32, 16, 128), BF),
            pltpu.VMEM((512, 128), F32),
            pltpu.VMEM((512, 128), F32),
            pltpu.VMEM((512, 256), F32),
            pltpu.VMEM((512, 256), F32),
            dma((2,)),
            dma((4,)),
            dma((4,)),
            dma((2, 2, 4, 2)),
            dma((2, 2, 4, 2)),
            dma((2, 16)),
            dma((16,)),
            dma((1,)),
            dma((1,)),
            dma((4, 32)),
            dma((4, 32)),
        ],
        compiler_params=pltpu.CompilerParams(collective_id=0, has_side_effects=True),
        name="mixer_backward",
    )(*operands)
    grad_query = product(mixed, conv_out)
    grad_key = product(grad_gated, value_in)
    grad_value = product(grad_gated, key_in)
    return (grad_query, grad_key, grad_value, filter_grad.reshape(4, 16384))


def solution(mesh):
    finer = Mesh(mesh.devices.reshape(16, 2, 4, 4, 2), CTX + MP)
    in_specs = (P(CTX, MP), P(MP, CTX), P(CTX, MP), P(CTX, MP), P(CTX, MP), P(EVERY, None))
    out_specs = (P(CTX, MP), P(CTX, MP), P(CTX, MP), P(EVERY, None))
    return jax.shard_map(body, mesh=finer, in_specs=in_specs, out_specs=out_specs, check_vma=False)
```

```python
import math

import jax
import jax.numpy as jnp
import ml_dtypes
import numpy as np
from jax import lax
from jax.experimental import pallas as pl
from jax.experimental.pallas import tpu as pltpu
from jax.sharding import Mesh
from jax.sharding import PartitionSpec as P

MESH = pl.DeviceIdType.MESH
CTX = ("zl", "core")
MP = ("y", "x", "zh")
EVERY = ("y", "x", "zh", "zl", "core")

BF = jnp.bfloat16
F32 = jnp.float32


def split_table(table):
    high = table.astype(np.float32).astype(ml_dtypes.bfloat16)
    low = (table - high.astype(np.float64)).astype(np.float32).astype(ml_dtypes.bfloat16)
    return (high, low)


def make_tables():
    size = 128
    order = np.arange(size).reshape(32, 4).T.reshape(-1)
    freq = np.arange(size) + 0.25
    angle_first = 2.0 * math.pi * np.outer(freq, order) / size
    first = np.concatenate([np.cos(angle_first), -np.sin(angle_first)], axis=0)
    angle_twist = 2.0 * math.pi * np.outer(freq, np.arange(size)) / (size * size)
    twist_re, twist_im = (np.cos(angle_twist), -np.sin(angle_twist))
    angle_second = 2.0 * math.pi * (np.outer(np.arange(size), np.arange(size)) % size) / size
    cos, sin = (np.cos(angle_second), np.sin(angle_second))
    second = np.block([[cos, -sin], [sin, cos]])
    second_back = np.block([[cos, sin], [-sin, cos]])
    first_back = np.concatenate([np.cos(angle_first).T, -np.sin(angle_first).T], axis=1) / (size * size)
    return (
        *split_table(first),
        twist_re.astype(np.float32),
        twist_im.astype(np.float32),
        *split_table(second),
        *split_table(second_back),
        *split_table(first_back),
    )


def dot(left, right):
    return lax.dot_general(left, right, (((1,), (0,)), ((), ())), preferred_element_type=F32)


def halves(values):
    high = values.astype(BF)
    return (high, (values - high.astype(F32)).astype(BF))


def table_dot(table, values, exact=False):
    if exact:
        high = values.astype(BF)
        return dot(table[0], high) + dot(table[1], high)
    high, low = halves(values)
    return dot(table[0], high) + (dot(table[1], high) + dot(table[0], low))


def dot_table(values, table):
    high, low = halves(values)
    return dot(high, table[0]) + (dot(high, table[1]) + dot(low, table[0]))


def forward(signals, first, twist, second, exact):
    spread = table_dot(first, jnp.concatenate(signals, axis=1), exact)
    rows = []
    for ch in range(4):
        re = spread[0:128, ch * 128 : ch * 128 + 128]
        im = spread[128:256, ch * 128 : ch * 128 + 128]
        turned = [re * twist[0] - im * twist[1], re * twist[1] + im * twist[0]]
        rows.append(jnp.concatenate(turned, axis=1))
    return dot_table(jnp.concatenate(rows, axis=0), second)


def backward(spec_re, spec_im, first_back, twist, second_back):
    gathered = dot_table(jnp.concatenate([spec_re, spec_im], axis=1), second_back)
    upper, lower = ([], [])
    for ch in range(4):
        re = gathered[ch * 128 : ch * 128 + 128, 0:128]
        im = gathered[ch * 128 : ch * 128 + 128, 128:256]
        upper.append(re * twist[0] + im * twist[1])
        lower.append(im * twist[0] - re * twist[1])
    stacked = jnp.concatenate([jnp.concatenate(upper, axis=1), jnp.concatenate(lower, axis=1)], axis=0)
    return table_dot(first_back, stacked)


def kernel(
    g, w, q_h, k_h, v_h, f_h, f1h_h, f1l_h, tre_h, tim_h, s2h_h, s2l_h, b2h_h, b2l_h, i1h_h, i1l_h,
    gm_o, conv_o, gg_o, fg_o,
    gbuf, wbuf, relay, sbuf, rbuf, rows, acc, fspec, gspec,
    q, k, v, f, f1h, f1l, tre, tim, s2h, s2l, b2h, b2l, i1h, i1l,
    loc_sem, in_sem, z_send, z_recv, p_send, p_recv, w_send, w_recv, a_send, a_recv,
):
    zl, core = (lax.axis_index("zl"), lax.axis_index("core"))
    y, x, zh = (lax.axis_index("y"), lax.axis_index("x"), lax.axis_index("zh"))
    me = zl * 2 + core
    x_up, x_dn, x_far = ((x + 1) % 4, (x + 3) % 4, (x + 2) % 4)
    y_up, y_dn, y_far = ((y + 1) % 4, (y + 3) % 4, (y + 2) % 4)
    z = zh * 16 + zl
    z_up, z_dn = ((z + 8) % 32, (z + 24) % 32)
    dev_up = {"zl": z_up % 16, "zh": z_up // 16}
    dev_dn = {"zl": z_dn % 16, "zh": z_dn // 16}
    other = 1 - zh

    def remote(src, dst, send, recv, dev):
        return pltpu.make_async_remote_copy(
            src_ref=src, dst_ref=dst, send_sem=send, recv_sem=recv, device_id=dev, device_id_type=MESH
        )

    barrier = pltpu.get_barrier_semaphore()
    dev_far_8, dev_far_4, dev_far_2, dev_far_1 = (
        {"zl": zl + d - 2 * d * (zl // d % 2)} for d in (8, 4, 2, 1)
    )
    for dev in (
        {"x": x_up}, {"x": x_dn}, {"y": y_up}, {"y": y_dn}, dev_up, dev_dn, {"core": 1 - core}, dev_far_4, dev_far_2, dev_far_1, dev_far_8
    ):
        pl.semaphore_signal(barrier, inc=1, device_id=dev, device_id_type=MESH)

    own_g = pltpu.make_async_copy(g, gbuf.at[zh, y, x], loc_sem.at[0])
    own_w = pltpu.make_async_copy(w, wbuf.at[core, zl], loc_sem.at[1])
    own_g.start()
    own_w.start()
    loads = [
        pltpu.make_async_copy(src, dst, in_sem.at[i])
        for i, (src, dst) in enumerate(
            (
                (k_h, k), (v_h, v), (q_h, q), (f_h, f), (f1h_h, f1h), (f1l_h, f1l), (tre_h, tre), (tim_h, tim),
                (s2h_h, s2h), (s2l_h, s2l), (b2h_h, b2h), (b2l_h, b2l), (i1h_h, i1h), (i1l_h, i1l),
            )
        )
    ]
    for load in loads:
        load.start()
    pl.semaphore_wait(barrier, 11)

    pending = []

    leg_up = remote(g.at[0:256], relay.at[0], z_send.at[0], z_recv.at[0], dev_up)
    leg_dn = remote(g.at[256:512], relay.at[1], z_send.at[1], z_recv.at[1], dev_dn)
    leg_up.start()
    leg_dn.start()
    pending += [leg_up, leg_dn]

    def second_legs():
        leg_up.wait_recv()
        leg_dn.wait_recv()
        on_up = remote(
            relay.at[0], gbuf.at[1 - z_up // 16, y, x, 0:256], z_send.at[2], z_recv.at[2], dev_up
        )
        on_dn = remote(
            relay.at[1], gbuf.at[1 - z_dn // 16, y, x, 256:512], z_send.at[3], z_recv.at[3], dev_dn
        )
        on_up.start()
        on_dn.start()
        pending.extend([on_up, on_dn])
        return (on_up, on_dn)

    def plane(slot, h):
        def low(yy, xx, start=0, size=256):
            return gbuf.at[slot, yy, xx, pl.ds(start, size)]

        def high(a, b, start=0, size=256):
            return gbuf.at[slot, a, b, pl.ds(256 + start, size)]

        ways = (
            (lambda a, b, *part: low(b, a, *part), x, x_dn, x_up, x_far, y, y_dn, y_up, "x", "y"),
            (lambda a, b, *part: high(a, b, *part), y, y_dn, y_up, y_far, x, x_dn, x_up, "y", "x"),
        )
        flying = {}

        def send(half, kind, way, ref, axis, index):
            copy = remote(ref, ref, p_send.at[h, half, kind, way], p_recv.at[h, half, kind, way], {axis: index})
            copy.start()
            pending.append(copy)
            flying[(half, kind, way)] = copy

        def got(half, kind, way):
            flying[(half, kind, way)].wait_recv()

        for half, (ref, a, a_dn, a_up, a_far, b, b_dn, b_up, ax, bx) in enumerate(ways):
            send(half, 0, 0, ref(a, b), ax, a_up)
            send(half, 0, 1, ref(a, b), ax, a_dn)
        for half, (ref, a, a_dn, a_up, a_far, b, b_dn, b_up, ax, bx) in enumerate(ways):
            send(half, 1, 0, ref(a, b), bx, b_up)
            send(half, 1, 1, ref(a, b), bx, b_dn)
        yield
        for half, (ref, a, a_dn, a_up, a_far, b, b_dn, b_up, ax, bx) in enumerate(ways):
            got(half, 0, 0)
            send(half, 2, 0, ref(a_dn, b, 0, 128), ax, a_up)
            got(half, 0, 1)
            send(half, 2, 1, ref(a_up, b, 128, 128), ax, a_dn)
        for half, (ref, a, a_dn, a_up, a_far, b, b_dn, b_up, ax, bx) in enumerate(ways):
            send(half, 3, 0, ref(a_dn, b), bx, b_up)
            send(half, 3, 1, ref(a_dn, b), bx, b_dn)
            send(half, 4, 0, ref(a_up, b), bx, b_up)
            send(half, 4, 1, ref(a_up, b), bx, b_dn)
        yield
        for half, (ref, a, a_dn, a_up, a_far, b, b_dn, b_up, ax, bx) in enumerate(ways):
            got(half, 1, 0)
            send(half, 6, 0, ref(a, b_dn), bx, b_up)
        for half, (ref, a, a_dn, a_up, a_far, b, b_dn, b_up, ax, bx) in enumerate(ways):
            got(half, 2, 0)
            got(half, 2, 1)
            send(half, 5, 0, ref(a_far, b), bx, b_up)
            send(half, 5, 1, ref(a_far, b), bx, b_dn)
        yield
        for half, (ref, a, a_dn, a_up, a_far, b, b_dn, b_up, ax, bx) in enumerate(ways):
            got(half, 4, 1)
            send(half, 6, 1, ref(a_up, b_up), bx, b_dn)
            got(half, 3, 0)
            send(half, 7, 0, ref(a_dn, b_dn), bx, b_up)
        yield
        for half, (ref, a, a_dn, a_up, a_far, b, b_dn, b_up, ax, bx) in enumerate(ways):
            got(half, 5, 1)
            send(half, 7, 1, ref(a_far, b_up), bx, b_dn)
        yield
        for half in range(2):
            for kind, way in ((1, 1), (3, 1), (4, 0), (5, 0), (6, 0), (6, 1), (7, 0), (7, 1)):
                got(half, kind, way)
        yield

    def block_at(d):
        return zl + sum(bit - 2 * bit * (zl // bit % 2) for bit in (8, 4, 2, 1) if d & bit)

    far_dev = {8: dev_far_8, 4: dev_far_4, 2: dev_far_2, 1: dev_far_1}
    w_copies = {}

    def hand_on(d):
        ref = wbuf.at[core, block_at(d)]
        if d:
            w_copies[d].wait_recv()
        for bit in (8, 4, 2, 1):
            if d & (2 * bit - 1) == 0:
                copy = remote(ref, ref, w_send.at[d + bit], w_recv.at[d + bit], far_dev[bit])
                copy.start()
                pending.append(copy)
                w_copies[d + bit] = copy

    def swap_rows():
        for d in range(1, 16, 2):
            w_copies[d].wait_recv()
        copy = remote(wbuf.at[core], wbuf.at[core], w_send.at[0], w_recv.at[0], {"core": 1 - core})
        copy.start()
        pending.append(copy)
        return copy

    def slab_copy(which, peer):
        return remote(
            sbuf.at[which, peer],
            rbuf.at[which, me],
            a_send.at[which, peer],
            a_recv.at[which, me],
            {"zl": peer // 2, "core": peer % 2},
        )

    def all_to_all_start(which):
        mine = pltpu.make_async_copy(sbuf.at[which, me], rbuf.at[which, me], a_recv.at[which, me])
        mine.start()

        def body(d, carry):
            slab_copy(which, (me + d) % 32).start()
            return carry

        lax.fori_loop(1, 32, body, 0)

    def all_to_all_wait(which):
        def body(d, carry):
            src = (me + d) % 32
            remote(
                sbuf.at[which, src], rbuf.at[which, src], a_send.at[which, src], a_recv.at[which, src],
                {"zl": src // 2, "core": src % 2},
            ).wait_recv()
            return carry

        lax.fori_loop(1, 32, body, 0)
        pltpu.make_async_copy(sbuf.at[which, me], rbuf.at[which, me], a_recv.at[which, me]).wait()

    def all_to_all_sent(which):
        def body(d, carry):
            slab_copy(which, (me + d) % 32).wait_send()
            return carry

        lax.fori_loop(1, 32, body, 0)

    def to_slabs(which, values):
        for p in range(4):
            rows[pl.ds(p, 128, stride=4), :] = values[p * 128 : p * 128 + 128, :].T
        sbuf[which] = rows[...].astype(BF).reshape(32, 16, 128)

    def from_slabs(which, out):
        rows[...] = rbuf[which].astype(F32).reshape(512, 128)
        for p in range(4):
            out[p * 128 : p * 128 + 128, :] = rows[pl.ds(p, 128, stride=4), :].T.astype(BF)

    def signals(which):
        rows[...] = rbuf[which].astype(F32).reshape(512, 128)
        return [
            jnp.concatenate([rows[pl.ds(ch * 4 + p, 32, stride=16), :] for p in range(4)], axis=0)
            for ch in range(4)
        ]

    def back_slabs(which, result):
        for ch in range(4):
            for p in range(4):
                rows[pl.ds(ch * 4 + p, 32, stride=16), :] = result[
                    p * 32 : p * 32 + 32, ch * 128 : ch * 128 + 128
                ]
        sbuf[which] = rows[...].astype(BF).reshape(32, 16, 128)

    def tables():
        return (
            (f1h[...], f1l[...]),
            (tre[...], tim[...]),
            (s2h[...], s2l[...]),
            (b2h[...], b2l[...]),
            (i1h[...], i1l[...]),
        )

    def multiply(slot):
        total = None
        for yy in range(4):
            for xx in range(4):
                part = lax.dot_general(
                    gbuf[slot, yy, xx],
                    wbuf[slot, yy * 4 + xx],
                    (((1,), (1,)), ((), ())),
                    preferred_element_type=F32,
                )
                total = part if total is None else total + part
        return total

    own_w.wait()
    hand_on(0)
    own_g.wait()
    own = plane(zh, 0)
    next(own)
    loads[0].wait()
    loads[1].wait()
    gated = (k[...].astype(F32) * v[...].astype(F32)).astype(BF).astype(F32)
    to_slabs(0, gated)
    hand_on(2)
    hand_on(4)
    hand_on(6)
    next(own)
    hand_on(8)
    hand_on(10)
    next(own)
    next(own)
    hand_on(12)
    hand_on(14)
    next(own)
    next(own)
    on_up, on_dn = second_legs()
    swap = swap_rows()
    swap.wait_recv()
    all_to_all_start(0)
    for load in loads[2:]:
        load.wait()
    first, twist, second, second_back, first_back = tables()
    acc[...] = multiply(zh)
    for n in range(128):
        rows[n * 4 : n * 4 + 4, :] = f[:, n * 128 : n * 128 + 128]
    filters = [
        jnp.concatenate([rows[pl.ds(p * 4 + ch, 32, stride=16), :] for p in range(4)], axis=0)
        for ch in range(4)
    ]
    fspec[...] = forward(filters, first, twist, second, False)
    on_up.wait_recv()
    on_dn.wait_recv()
    rest = plane(other, 1)
    next(rest)
    next(rest)
    next(rest)
    next(rest)
    next(rest)
    next(rest)
    mixed = (acc[...] + multiply(other)).astype(BF)
    gm_o[...] = mixed
    to_slabs(1, mixed.astype(F32) * q[...].astype(F32))
    all_to_all_start(1)
    all_to_all_wait(0)
    gspec[...] = forward(signals(0), first, twist, second, True)
    f_re, f_im = (fspec[:, 0:128], fspec[:, 128:256])
    g_re, g_im = (gspec[:, 0:128], gspec[:, 128:256])
    back_slabs(
        2, backward(f_re * g_re - f_im * g_im, f_re * g_im + f_im * g_re, first_back, twist, second_back)
    )
    all_to_all_start(2)
    all_to_all_wait(1)
    spec = forward(signals(1), first, twist, second, True)
    s_re, s_im = (spec[:, 0:128], spec[:, 128:256])
    f_re, f_im = (fspec[:, 0:128], fspec[:, 128:256])
    back_slabs(
        3, backward(s_re * f_re + s_im * f_im, s_im * f_re - s_re * f_im, first_back, twist, second_back)
    )
    all_to_all_start(3)
    g_re, g_im = (gspec[:, 0:128], gspec[:, 128:256])
    lags = backward(s_re * g_re + s_im * g_im, s_im * g_re - s_re * g_im, first_back, twist, second_back)
    for ch in range(4):
        for p in range(4):
            fg_o[ch, pl.ds(p, 32, stride=4), :] = (
                lags[p * 32 : p * 32 + 32, ch * 128 : ch * 128 + 128] * (1.0 / 128.0)
            )
    all_to_all_wait(2)
    from_slabs(2, conv_o)
    all_to_all_wait(3)
    from_slabs(3, gg_o)

    for copy in pending:
        copy.wait_send()
    for which in range(4):
        all_to_all_sent(which)


def product(left, right):
    return (left.astype(F32) * right.astype(F32)).astype(BF)


def body(grad_out, proj_out, query, key_in, value_in, filters):
    tables = make_tables()
    operands = (grad_out, proj_out, query, key_in, value_in, filters, *tables)
    tile = jax.ShapeDtypeStruct((512, 128), BF)
    vmem = pl.BlockSpec(memory_space=pltpu.VMEM)
    far = pl.BlockSpec(memory_space=pl.ANY)
    dma = pltpu.SemaphoreType.DMA
    mixed, conv_out, grad_gated, filter_grad = pl.pallas_call(
        kernel,
        out_shape=(tile, tile, tile, jax.ShapeDtypeStruct((4, 128, 128), F32)),
        in_specs=[far] * len(operands),
        out_specs=(vmem,) * 4,
        scratch_shapes=[
            pltpu.VMEM((2, 4, 4, 512, 128), BF),
            pltpu.VMEM((2, 16, 128, 128), BF),
            pltpu.VMEM((2, 256, 128), BF),
            pltpu.VMEM((4, 32, 16, 128), BF),
            pltpu.VMEM((4, 32, 16, 128), BF),
            pltpu.VMEM((512, 128), F32),
            pltpu.VMEM((512, 128), F32),
            pltpu.VMEM((512, 256), F32),
            pltpu.VMEM((512, 256), F32),
            *(pltpu.VMEM(operand.shape, operand.dtype) for operand in operands[2:]),
            dma((2,)),
            dma((14,)),
            dma((4,)),
            dma((4,)),
            dma((2, 2, 8, 2)),
            dma((2, 2, 8, 2)),
            dma((16,)),
            dma((16,)),
            dma((4, 32)),
            dma((4, 32)),
        ],
        compiler_params=pltpu.CompilerParams(collective_id=0, has_side_effects=True),
        name="mixer_backward",
    )(*operands)
    grad_query = product(mixed, conv_out)
    grad_key = product(grad_gated, value_in)
    grad_value = product(grad_gated, key_in)
    return (grad_query, grad_key, grad_value, filter_grad.reshape(4, 16384))


def solution(mesh):
    finer = Mesh(mesh.devices.reshape(16, 2, 4, 4, 2), CTX + MP)
    in_specs = (P(CTX, MP), P(MP, CTX), P(CTX, MP), P(CTX, MP), P(CTX, MP), P(EVERY, None))
    out_specs = (P(CTX, MP), P(CTX, MP), P(CTX, MP), P(EVERY, None))
    return jax.shard_map(body, mesh=finer, in_specs=in_specs, out_specs=out_specs, check_vma=False)
```

```python
import math

import jax
import jax.numpy as jnp
import ml_dtypes
import numpy as np
from jax import lax
from jax.experimental import pallas as pl
from jax.experimental.pallas import tpu as pltpu
from jax.sharding import Mesh
from jax.sharding import PartitionSpec as P

MESH = pl.DeviceIdType.MESH
CTX = ("zl", "core")
MP = ("y", "x", "zh")
EVERY = ("y", "x", "zh", "zl", "core")

BF = jnp.bfloat16
F32 = jnp.float32


def split_table(table):
    high = table.astype(np.float32).astype(ml_dtypes.bfloat16)
    low = (table - high.astype(np.float64)).astype(np.float32).astype(ml_dtypes.bfloat16)
    return (high, low)


def make_tables():
    size = 128
    order = np.arange(size).reshape(32, 4).T.reshape(-1)
    freq = np.arange(size) + 0.25
    angle_first = 2.0 * math.pi * np.outer(freq, order) / size
    first = np.concatenate([np.cos(angle_first), -np.sin(angle_first)], axis=0)
    angle_twist = 2.0 * math.pi * np.outer(freq, np.arange(size)) / (size * size)
    twist_re, twist_im = (np.cos(angle_twist), -np.sin(angle_twist))
    angle_second = 2.0 * math.pi * (np.outer(np.arange(size), np.arange(size)) % size) / size
    cos, sin = (np.cos(angle_second), np.sin(angle_second))
    second = np.block([[cos, -sin], [sin, cos]])
    second_back = np.block([[cos, sin], [-sin, cos]])
    first_back = np.concatenate([np.cos(angle_first).T, -np.sin(angle_first).T], axis=1) / (size * size)
    return (
        *split_table(first),
        twist_re.astype(np.float32),
        twist_im.astype(np.float32),
        *split_table(second),
        *split_table(second_back),
        *split_table(first_back),
    )


def dot(left, right):
    return lax.dot_general(left, right, (((1,), (0,)), ((), ())), preferred_element_type=F32)


def halves(values):
    high = values.astype(BF)
    return (high, (values - high.astype(F32)).astype(BF))


def table_dot(table, values, exact=False):
    if exact:
        high = values.astype(BF)
        return dot(table[0], high) + dot(table[1], high)
    high, low = halves(values)
    return dot(table[0], high) + (dot(table[1], high) + dot(table[0], low))


def dot_table(values, table):
    high, low = halves(values)
    return dot(high, table[0]) + (dot(high, table[1]) + dot(low, table[0]))


def forward(signals, first, twist, second, exact):
    spread = table_dot(first, jnp.concatenate(signals, axis=1), exact)
    rows = []
    for ch in range(4):
        re = spread[0:128, ch * 128 : ch * 128 + 128]
        im = spread[128:256, ch * 128 : ch * 128 + 128]
        turned = [re * twist[0] - im * twist[1], re * twist[1] + im * twist[0]]
        rows.append(jnp.concatenate(turned, axis=1))
    return dot_table(jnp.concatenate(rows, axis=0), second)


def backward(spec_re, spec_im, first_back, twist, second_back):
    gathered = dot_table(jnp.concatenate([spec_re, spec_im], axis=1), second_back)
    upper, lower = ([], [])
    for ch in range(4):
        re = gathered[ch * 128 : ch * 128 + 128, 0:128]
        im = gathered[ch * 128 : ch * 128 + 128, 128:256]
        upper.append(re * twist[0] + im * twist[1])
        lower.append(im * twist[0] - re * twist[1])
    stacked = jnp.concatenate([jnp.concatenate(upper, axis=1), jnp.concatenate(lower, axis=1)], axis=0)
    return table_dot(first_back, stacked)


def kernel(
    g, w, q_h, k_h, v_h, f_h, f1h_h, f1l_h, tre_h, tim_h, s2h_h, s2l_h, b2h_h, b2l_h, i1h_h, i1l_h,
    gm_o, conv_o, gg_o, fg_o,
    gbuf, wbuf, relay, sbuf, rbuf, rows, acc, fspec, gspec,
    q, k, v, f, f1h, f1l, tre, tim, s2h, s2l, b2h, b2l, i1h, i1l,
    loc_sem, in_sem, z_send, z_recv, p_send, p_recv, w_send, w_recv, a_send, a_recv,
):
    zl, core = (lax.axis_index("zl"), lax.axis_index("core"))
    y, x, zh = (lax.axis_index("y"), lax.axis_index("x"), lax.axis_index("zh"))
    me = zl * 2 + core
    x_up, x_dn, x_far = ((x + 1) % 4, (x + 3) % 4, (x + 2) % 4)
    y_up, y_dn, y_far = ((y + 1) % 4, (y + 3) % 4, (y + 2) % 4)
    z = zh * 16 + zl
    z_up, z_dn = ((z + 8) % 32, (z + 24) % 32)
    dev_up = {"zl": z_up % 16, "zh": z_up // 16}
    dev_dn = {"zl": z_dn % 16, "zh": z_dn // 16}
    other = 1 - zh

    def remote(src, dst, send, recv, dev):
        return pltpu.make_async_remote_copy(
            src_ref=src, dst_ref=dst, send_sem=send, recv_sem=recv, device_id=dev, device_id_type=MESH
        )

    barrier = pltpu.get_barrier_semaphore()
    dev_far_8, dev_far_4, dev_far_2, dev_far_1 = (
        {"zl": zl + d - 2 * d * (zl // d % 2)} for d in (8, 4, 2, 1)
    )
    for dev in (
        {"x": x_up}, {"x": x_dn}, {"y": y_up}, {"y": y_dn}, dev_up, dev_dn, {"core": 1 - core}, dev_far_4, dev_far_2, dev_far_1, dev_far_8
    ):
        pl.semaphore_signal(barrier, inc=1, device_id=dev, device_id_type=MESH)

    own_g = pltpu.make_async_copy(g, gbuf.at[zh, y, x], loc_sem.at[0])
    own_w = pltpu.make_async_copy(w, wbuf.at[core, zl], loc_sem.at[1])
    own_g.start()
    own_w.start()
    loads = [
        pltpu.make_async_copy(src, dst, in_sem.at[i])
        for i, (src, dst) in enumerate(
            (
                (k_h, k), (v_h, v), (q_h, q), (f_h, f), (f1h_h, f1h), (f1l_h, f1l), (tre_h, tre), (tim_h, tim),
                (s2h_h, s2h), (s2l_h, s2l), (b2h_h, b2h), (b2l_h, b2l), (i1h_h, i1h), (i1l_h, i1l),
            )
        )
    ]
    for load in loads:
        load.start()
    pl.semaphore_wait(barrier, 11)

    pending = []

    leg_up = remote(g.at[0:256], relay.at[0], z_send.at[0], z_recv.at[0], dev_up)
    leg_dn = remote(g.at[256:512], relay.at[1], z_send.at[1], z_recv.at[1], dev_dn)
    leg_up.start()
    leg_dn.start()
    pending += [leg_up, leg_dn]

    def second_legs():
        leg_up.wait_recv()
        leg_dn.wait_recv()
        on_up = remote(
            relay.at[0], gbuf.at[1 - z_up // 16, y, x, 0:256], z_send.at[2], z_recv.at[2], dev_up
        )
        on_dn = remote(
            relay.at[1], gbuf.at[1 - z_dn // 16, y, x, 256:512], z_send.at[3], z_recv.at[3], dev_dn
        )
        on_up.start()
        on_dn.start()
        pending.extend([on_up, on_dn])
        return (on_up, on_dn)

    def plane(slot, h):
        def low(yy, xx, start=0, size=256):
            return gbuf.at[slot, yy, xx, pl.ds(start, size)]

        def high(a, b, start=0, size=256):
            return gbuf.at[slot, a, b, pl.ds(256 + start, size)]

        ways = (
            (lambda a, b, *part: low(b, a, *part), x, x_dn, x_up, x_far, y, y_dn, y_up, "x", "y"),
            (lambda a, b, *part: high(a, b, *part), y, y_dn, y_up, y_far, x, x_dn, x_up, "y", "x"),
        )
        flying = {}

        def send(half, kind, way, ref, axis, index):
            copy = remote(ref, ref, p_send.at[h, half, kind, way], p_recv.at[h, half, kind, way], {axis: index})
            copy.start()
            pending.append(copy)
            flying[(half, kind, way)] = copy

        def got(half, kind, way):
            flying[(half, kind, way)].wait_recv()

        for half, (ref, a, a_dn, a_up, a_far, b, b_dn, b_up, ax, bx) in enumerate(ways):
            send(half, 0, 0, ref(a, b), ax, a_up)
            send(half, 0, 1, ref(a, b), ax, a_dn)
        for half, (ref, a, a_dn, a_up, a_far, b, b_dn, b_up, ax, bx) in enumerate(ways):
            send(half, 1, 0, ref(a, b), bx, b_up)
            send(half, 1, 1, ref(a, b), bx, b_dn)
        yield
        for half, (ref, a, a_dn, a_up, a_far, b, b_dn, b_up, ax, bx) in enumerate(ways):
            got(half, 0, 0)
            send(half, 2, 0, ref(a_dn, b, 0, 128), ax, a_up)
            got(half, 0, 1)
            send(half, 2, 1, ref(a_up, b, 128, 128), ax, a_dn)
        for half, (ref, a, a_dn, a_up, a_far, b, b_dn, b_up, ax, bx) in enumerate(ways):
            send(half, 3, 0, ref(a_dn, b), bx, b_up)
            send(half, 3, 1, ref(a_dn, b), bx, b_dn)
            send(half, 4, 0, ref(a_up, b), bx, b_up)
            send(half, 4, 1, ref(a_up, b), bx, b_dn)
        yield
        for half, (ref, a, a_dn, a_up, a_far, b, b_dn, b_up, ax, bx) in enumerate(ways):
            got(half, 1, 0)
            send(half, 6, 0, ref(a, b_dn), bx, b_up)
        for half, (ref, a, a_dn, a_up, a_far, b, b_dn, b_up, ax, bx) in enumerate(ways):
            got(half, 2, 0)
            got(half, 2, 1)
            send(half, 5, 0, ref(a_far, b), bx, b_up)
            send(half, 5, 1, ref(a_far, b), bx, b_dn)
        yield
        for half, (ref, a, a_dn, a_up, a_far, b, b_dn, b_up, ax, bx) in enumerate(ways):
            got(half, 4, 1)
            send(half, 6, 1, ref(a_up, b_up), bx, b_dn)
            got(half, 3, 0)
            send(half, 7, 0, ref(a_dn, b_dn), bx, b_up)
        yield
        for half, (ref, a, a_dn, a_up, a_far, b, b_dn, b_up, ax, bx) in enumerate(ways):
            got(half, 5, 1)
            send(half, 7, 1, ref(a_far, b_up), bx, b_dn)
        yield
        for half in range(2):
            for kind, way in ((1, 1), (3, 1), (4, 0), (5, 0), (6, 0), (6, 1), (7, 0), (7, 1)):
                got(half, kind, way)
        yield

    def block_at(d):
        return zl + sum(bit - 2 * bit * (zl // bit % 2) for bit in (8, 4, 2, 1) if d & bit)

    far_dev = {8: dev_far_8, 4: dev_far_4, 2: dev_far_2, 1: dev_far_1}
    w_copies = {}

    def hand_on(d):
        ref = wbuf.at[core, block_at(d)]
        if d:
            w_copies[d].wait_recv()
        for bit in (8, 4, 2, 1):
            if d & (2 * bit - 1) == 0:
                copy = remote(ref, ref, w_send.at[d + bit], w_recv.at[d + bit], far_dev[bit])
                copy.start()
                pending.append(copy)
                w_copies[d + bit] = copy

    def swap_rows():
        for d in range(1, 16, 2):
            w_copies[d].wait_recv()
        copy = remote(wbuf.at[core], wbuf.at[core], w_send.at[0], w_recv.at[0], {"core": 1 - core})
        copy.start()
        pending.append(copy)
        return copy

    def slab_copy(which, peer):
        return remote(
            sbuf.at[which, peer],
            rbuf.at[which, me],
            a_send.at[which, peer],
            a_recv.at[which, me],
            {"zl": peer // 2, "core": peer % 2},
        )

    def all_to_all_start(which):
        mine = pltpu.make_async_copy(sbuf.at[which, me], rbuf.at[which, me], a_recv.at[which, me])
        mine.start()

        def body(d, carry):
            slab_copy(which, (me + d) % 32).start()
            return carry

        lax.fori_loop(1, 32, body, 0)

    def all_to_all_wait(which):
        def body(d, carry):
            src = (me + d) % 32
            remote(
                sbuf.at[which, src], rbuf.at[which, src], a_send.at[which, src], a_recv.at[which, src],
                {"zl": src // 2, "core": src % 2},
            ).wait_recv()
            return carry

        lax.fori_loop(1, 32, body, 0)
        pltpu.make_async_copy(sbuf.at[which, me], rbuf.at[which, me], a_recv.at[which, me]).wait()

    def all_to_all_sent(which):
        def body(d, carry):
            slab_copy(which, (me + d) % 32).wait_send()
            return carry

        lax.fori_loop(1, 32, body, 0)

    def to_slabs(which, values):
        for p in range(4):
            rows[pl.ds(p, 128, stride=4), :] = values[p * 128 : p * 128 + 128, :].T
        sbuf[which] = rows[...].astype(BF).reshape(32, 16, 128)

    def from_slabs(which, out):
        rows[...] = rbuf[which].astype(F32).reshape(512, 128)
        for p in range(4):
            out[p * 128 : p * 128 + 128, :] = rows[pl.ds(p, 128, stride=4), :].T.astype(BF)

    def signals(which):
        rows[...] = rbuf[which].astype(F32).reshape(512, 128)
        return [
            jnp.concatenate([rows[pl.ds(ch * 4 + p, 32, stride=16), :] for p in range(4)], axis=0)
            for ch in range(4)
        ]

    def back_slabs(which, result):
        for ch in range(4):
            for p in range(4):
                rows[pl.ds(ch * 4 + p, 32, stride=16), :] = result[
                    p * 32 : p * 32 + 32, ch * 128 : ch * 128 + 128
                ]
        sbuf[which] = rows[...].astype(BF).reshape(32, 16, 128)

    def tables():
        return (
            (f1h[...], f1l[...]),
            (tre[...], tim[...]),
            (s2h[...], s2l[...]),
            (b2h[...], b2l[...]),
            (i1h[...], i1l[...]),
        )

    def multiply(slot):
        total = None
        for yy in range(4):
            for xx in range(4):
                part = lax.dot_general(
                    gbuf[slot, yy, xx],
                    wbuf[slot, yy * 4 + xx],
                    (((1,), (1,)), ((), ())),
                    preferred_element_type=F32,
                )
                total = part if total is None else total + part
        return total

    own_w.wait()
    hand_on(0)
    own_g.wait()
    own = plane(zh, 0)
    next(own)
    loads[0].wait()
    loads[1].wait()
    gated = (k[...].astype(F32) * v[...].astype(F32)).astype(BF).astype(F32)
    to_slabs(0, gated)
    next(own)
    next(own)
    next(own)
    on_up, on_dn = second_legs()
    next(own)
    next(own)
    hand_on(2)
    hand_on(4)
    hand_on(6)
    hand_on(8)
    for load in loads[2:]:
        load.wait()
    first, twist, second, second_back, first_back = tables()
    on_up.wait_recv()
    on_dn.wait_recv()
    rest = plane(other, 1)
    next(rest)
    next(rest)
    hand_on(10)
    hand_on(12)
    hand_on(14)
    next(rest)
    swap = swap_rows()
    swap.wait_recv()
    all_to_all_start(0)
    acc[...] = multiply(zh)
    for n in range(128):
        rows[n * 4 : n * 4 + 4, :] = f[:, n * 128 : n * 128 + 128]
    filters = [
        jnp.concatenate([rows[pl.ds(p * 4 + ch, 32, stride=16), :] for p in range(4)], axis=0)
        for ch in range(4)
    ]
    fspec[...] = forward(filters, first, twist, second, False)
    next(rest)
    next(rest)
    next(rest)
    mixed = (acc[...] + multiply(other)).astype(BF)
    gm_o[...] = mixed
    to_slabs(1, mixed.astype(F32) * q[...].astype(F32))
    all_to_all_start(1)
    all_to_all_wait(0)
    gspec[...] = forward(signals(0), first, twist, second, True)
    f_re, f_im = (fspec[:, 0:128], fspec[:, 128:256])
    g_re, g_im = (gspec[:, 0:128], gspec[:, 128:256])
    back_slabs(
        2, backward(f_re * g_re - f_im * g_im, f_re * g_im + f_im * g_re, first_back, twist, second_back)
    )
    all_to_all_start(2)
    all_to_all_wait(1)
    spec = forward(signals(1), first, twist, second, True)
    s_re, s_im = (spec[:, 0:128], spec[:, 128:256])
    f_re, f_im = (fspec[:, 0:128], fspec[:, 128:256])
    back_slabs(
        3, backward(s_re * f_re + s_im * f_im, s_im * f_re - s_re * f_im, first_back, twist, second_back)
    )
    all_to_all_start(3)
    g_re, g_im = (gspec[:, 0:128], gspec[:, 128:256])
    lags = backward(s_re * g_re + s_im * g_im, s_im * g_re - s_re * g_im, first_back, twist, second_back)
    for ch in range(4):
        for p in range(4):
            fg_o[ch, pl.ds(p, 32, stride=4), :] = (
                lags[p * 32 : p * 32 + 32, ch * 128 : ch * 128 + 128] * (1.0 / 128.0)
            )
    all_to_all_wait(2)
    from_slabs(2, conv_o)
    all_to_all_wait(3)
    from_slabs(3, gg_o)

    for copy in pending:
        copy.wait_send()
    for which in range(4):
        all_to_all_sent(which)


def product(left, right):
    return (left.astype(F32) * right.astype(F32)).astype(BF)


def body(grad_out, proj_out, query, key_in, value_in, filters):
    tables = make_tables()
    operands = (grad_out, proj_out, query, key_in, value_in, filters, *tables)
    tile = jax.ShapeDtypeStruct((512, 128), BF)
    vmem = pl.BlockSpec(memory_space=pltpu.VMEM)
    far = pl.BlockSpec(memory_space=pl.ANY)
    dma = pltpu.SemaphoreType.DMA
    mixed, conv_out, grad_gated, filter_grad = pl.pallas_call(
        kernel,
        out_shape=(tile, tile, tile, jax.ShapeDtypeStruct((4, 128, 128), F32)),
        in_specs=[far] * len(operands),
        out_specs=(vmem,) * 4,
        scratch_shapes=[
            pltpu.VMEM((2, 4, 4, 512, 128), BF),
            pltpu.VMEM((2, 16, 128, 128), BF),
            pltpu.VMEM((2, 256, 128), BF),
            pltpu.VMEM((4, 32, 16, 128), BF),
            pltpu.VMEM((4, 32, 16, 128), BF),
            pltpu.VMEM((512, 128), F32),
            pltpu.VMEM((512, 128), F32),
            pltpu.VMEM((512, 256), F32),
            pltpu.VMEM((512, 256), F32),
            *(pltpu.VMEM(operand.shape, operand.dtype) for operand in operands[2:]),
            dma((2,)),
            dma((14,)),
            dma((4,)),
            dma((4,)),
            dma((2, 2, 8, 2)),
            dma((2, 2, 8, 2)),
            dma((16,)),
            dma((16,)),
            dma((4, 32)),
            dma((4, 32)),
        ],
        compiler_params=pltpu.CompilerParams(collective_id=0, has_side_effects=True),
        name="mixer_backward",
    )(*operands)
    grad_query = product(mixed, conv_out)
    grad_key = product(grad_gated, value_in)
    grad_value = product(grad_gated, key_in)
    return (grad_query, grad_key, grad_value, filter_grad.reshape(4, 16384))


def solution(mesh):
    finer = Mesh(mesh.devices.reshape(16, 2, 4, 4, 2), CTX + MP)
    in_specs = (P(CTX, MP), P(MP, CTX), P(CTX, MP), P(CTX, MP), P(CTX, MP), P(EVERY, None))
    out_specs = (P(CTX, MP), P(CTX, MP), P(CTX, MP), P(EVERY, None))
    return jax.shard_map(body, mesh=finer, in_specs=in_specs, out_specs=out_specs, check_vma=False)
```

```python
import math

import jax
import jax.numpy as jnp
import ml_dtypes
import numpy as np
from jax import lax
from jax.experimental import pallas as pl
from jax.experimental.pallas import tpu as pltpu
from jax.sharding import Mesh
from jax.sharding import PartitionSpec as P

MESH = pl.DeviceIdType.MESH
CTX = ("zl", "core")
MP = ("y", "x", "zh")
EVERY = ("y", "x", "zh", "zl", "core")

BF = jnp.bfloat16
F32 = jnp.float32


def split_table(table):
    high = table.astype(np.float32).astype(ml_dtypes.bfloat16)
    low = (table - high.astype(np.float64)).astype(np.float32).astype(ml_dtypes.bfloat16)
    return (high, low)


def make_tables():
    size = 128
    order = np.arange(size).reshape(32, 4).T.reshape(-1)
    freq = np.arange(size) + 0.25
    angle_first = 2.0 * math.pi * np.outer(freq, order) / size
    first = np.concatenate([np.cos(angle_first), -np.sin(angle_first)], axis=0)
    angle_twist = 2.0 * math.pi * np.outer(freq, np.arange(size)) / (size * size)
    twist_re, twist_im = (np.cos(angle_twist), -np.sin(angle_twist))
    angle_second = 2.0 * math.pi * (np.outer(np.arange(size), np.arange(size)) % size) / size
    cos, sin = (np.cos(angle_second), np.sin(angle_second))
    second = np.block([[cos, -sin], [sin, cos]])
    second_back = np.block([[cos, sin], [-sin, cos]])
    first_back = np.concatenate([np.cos(angle_first).T, -np.sin(angle_first).T], axis=1) / (size * size)
    return (
        *split_table(first),
        twist_re.astype(np.float32),
        twist_im.astype(np.float32),
        *split_table(second),
        *split_table(second_back),
        *split_table(first_back),
    )


def dot(left, right):
    return lax.dot_general(left, right, (((1,), (0,)), ((), ())), preferred_element_type=F32)


def halves(values):
    high = values.astype(BF)
    return (high, (values - high.astype(F32)).astype(BF))


def table_dot(table, values, exact=False):
    if exact:
        high = values.astype(BF)
        return dot(table[0], high) + dot(table[1], high)
    high, low = halves(values)
    return dot(table[0], high) + (dot(table[1], high) + dot(table[0], low))


def dot_table(values, table):
    high, low = halves(values)
    return dot(high, table[0]) + (dot(high, table[1]) + dot(low, table[0]))


def forward(signals, first, twist, second, exact):
    spread = table_dot(first, jnp.concatenate(signals, axis=1), exact)
    rows = []
    for ch in range(4):
        re = spread[0:128, ch * 128 : ch * 128 + 128]
        im = spread[128:256, ch * 128 : ch * 128 + 128]
        turned = [re * twist[0] - im * twist[1], re * twist[1] + im * twist[0]]
        rows.append(jnp.concatenate(turned, axis=1))
    return dot_table(jnp.concatenate(rows, axis=0), second)


def backward(spec_re, spec_im, first_back, twist, second_back):
    gathered = dot_table(jnp.concatenate([spec_re, spec_im], axis=1), second_back)
    upper, lower = ([], [])
    for ch in range(4):
        re = gathered[ch * 128 : ch * 128 + 128, 0:128]
        im = gathered[ch * 128 : ch * 128 + 128, 128:256]
        upper.append(re * twist[0] + im * twist[1])
        lower.append(im * twist[0] - re * twist[1])
    stacked = jnp.concatenate([jnp.concatenate(upper, axis=1), jnp.concatenate(lower, axis=1)], axis=0)
    return table_dot(first_back, stacked)


def kernel(
    g, w, q_h, k_h, v_h, f_h, f1h_h, f1l_h, tre_h, tim_h, s2h_h, s2l_h, b2h_h, b2l_h, i1h_h, i1l_h,
    gm_h, conv_h, gg_o, fg_h,
    gbuf, wbuf, relay, sbuf, rbuf, rows, acc, fspec, gspec,
    q, k, v, f, f1h, f1l, tre, tim, s2h, s2l, b2h, b2l, i1h, i1l,
    loc_sem, in_sem, z_send, z_recv, p_send, p_recv, w_send, w_recv, a_send, a_recv, gm_o, conv_o, fg_o, out_sem,
):
    zl, core = (lax.axis_index("zl"), lax.axis_index("core"))
    y, x, zh = (lax.axis_index("y"), lax.axis_index("x"), lax.axis_index("zh"))
    me = zl * 2 + core
    x_up, x_dn, x_far = ((x + 1) % 4, (x + 3) % 4, (x + 2) % 4)
    y_up, y_dn, y_far = ((y + 1) % 4, (y + 3) % 4, (y + 2) % 4)
    z = zh * 16 + zl
    z_up, z_dn = ((z + 8) % 32, (z + 24) % 32)
    dev_up = {"zl": z_up % 16, "zh": z_up // 16}
    dev_dn = {"zl": z_dn % 16, "zh": z_dn // 16}
    other = 1 - zh

    def remote(src, dst, send, recv, dev):
        return pltpu.make_async_remote_copy(
            src_ref=src, dst_ref=dst, send_sem=send, recv_sem=recv, device_id=dev, device_id_type=MESH
        )

    barrier = pltpu.get_barrier_semaphore()
    dev_far_8, dev_far_4, dev_far_2, dev_far_1 = (
        {"zl": zl + d - 2 * d * (zl // d % 2)} for d in (8, 4, 2, 1)
    )
    for dev in (
        {"x": x_up}, {"x": x_dn}, {"y": y_up}, {"y": y_dn}, dev_up, dev_dn, {"core": 1 - core}, dev_far_4, dev_far_2, dev_far_1, dev_far_8
    ):
        pl.semaphore_signal(barrier, inc=1, device_id=dev, device_id_type=MESH)

    own_g = pltpu.make_async_copy(g, gbuf.at[zh, y, x], loc_sem.at[0])
    own_w = pltpu.make_async_copy(w, wbuf.at[core, zl], loc_sem.at[1])
    own_g.start()
    own_w.start()
    loads = [
        pltpu.make_async_copy(src, dst, in_sem.at[i])
        for i, (src, dst) in enumerate(
            (
                (k_h, k), (v_h, v), (q_h, q), (f_h, f), (f1h_h, f1h), (f1l_h, f1l), (tre_h, tre), (tim_h, tim),
                (s2h_h, s2h), (s2l_h, s2l), (b2h_h, b2h), (b2l_h, b2l), (i1h_h, i1h), (i1l_h, i1l),
            )
        )
    ]
    for load in loads:
        load.start()
    pl.semaphore_wait(barrier, 11)

    pending = []

    leg_up = remote(g.at[0:256], relay.at[0], z_send.at[0], z_recv.at[0], dev_up)
    leg_dn = remote(g.at[256:512], relay.at[1], z_send.at[1], z_recv.at[1], dev_dn)
    leg_up.start()
    leg_dn.start()
    pending += [leg_up, leg_dn]

    def second_legs():
        leg_up.wait_recv()
        leg_dn.wait_recv()
        on_up = remote(
            relay.at[0], gbuf.at[1 - z_up // 16, y, x, 0:256], z_send.at[2], z_recv.at[2], dev_up
        )
        on_dn = remote(
            relay.at[1], gbuf.at[1 - z_dn // 16, y, x, 256:512], z_send.at[3], z_recv.at[3], dev_dn
        )
        on_up.start()
        on_dn.start()
        pending.extend([on_up, on_dn])
        return (on_up, on_dn)

    def plane(slot, h):
        def low(yy, xx, start=0, size=256):
            return gbuf.at[slot, yy, xx, pl.ds(start, size)]

        def high(a, b, start=0, size=256):
            return gbuf.at[slot, a, b, pl.ds(256 + start, size)]

        ways = (
            (lambda a, b, *part: low(b, a, *part), x, x_dn, x_up, x_far, y, y_dn, y_up, "x", "y"),
            (lambda a, b, *part: high(a, b, *part), y, y_dn, y_up, y_far, x, x_dn, x_up, "y", "x"),
        )
        flying = {}

        def send(half, kind, way, ref, axis, index):
            copy = remote(ref, ref, p_send.at[h, half, kind, way], p_recv.at[h, half, kind, way], {axis: index})
            copy.start()
            pending.append(copy)
            flying[(half, kind, way)] = copy

        def got(half, kind, way):
            flying[(half, kind, way)].wait_recv()

        for half, (ref, a, a_dn, a_up, a_far, b, b_dn, b_up, ax, bx) in enumerate(ways):
            send(half, 0, 0, ref(a, b), ax, a_up)
            send(half, 0, 1, ref(a, b), ax, a_dn)
        for half, (ref, a, a_dn, a_up, a_far, b, b_dn, b_up, ax, bx) in enumerate(ways):
            send(half, 1, 0, ref(a, b), bx, b_up)
            send(half, 1, 1, ref(a, b), bx, b_dn)
        yield
        for half, (ref, a, a_dn, a_up, a_far, b, b_dn, b_up, ax, bx) in enumerate(ways):
            got(half, 0, 0)
            send(half, 2, 0, ref(a_dn, b, 0, 128), ax, a_up)
            got(half, 0, 1)
            send(half, 2, 1, ref(a_up, b, 128, 128), ax, a_dn)
        for half, (ref, a, a_dn, a_up, a_far, b, b_dn, b_up, ax, bx) in enumerate(ways):
            send(half, 3, 0, ref(a_dn, b), bx, b_up)
            send(half, 3, 1, ref(a_dn, b), bx, b_dn)
            send(half, 4, 0, ref(a_up, b), bx, b_up)
            send(half, 4, 1, ref(a_up, b), bx, b_dn)
        yield
        for half, (ref, a, a_dn, a_up, a_far, b, b_dn, b_up, ax, bx) in enumerate(ways):
            got(half, 1, 0)
            send(half, 6, 0, ref(a, b_dn), bx, b_up)
        for half, (ref, a, a_dn, a_up, a_far, b, b_dn, b_up, ax, bx) in enumerate(ways):
            got(half, 2, 0)
            got(half, 2, 1)
            send(half, 5, 0, ref(a_far, b), bx, b_up)
            send(half, 5, 1, ref(a_far, b), bx, b_dn)
        yield
        for half, (ref, a, a_dn, a_up, a_far, b, b_dn, b_up, ax, bx) in enumerate(ways):
            got(half, 4, 1)
            send(half, 6, 1, ref(a_up, b_up), bx, b_dn)
            got(half, 3, 0)
            send(half, 7, 0, ref(a_dn, b_dn), bx, b_up)
        yield
        for half, (ref, a, a_dn, a_up, a_far, b, b_dn, b_up, ax, bx) in enumerate(ways):
            got(half, 5, 1)
            send(half, 7, 1, ref(a_far, b_up), bx, b_dn)
        yield
        for half in range(2):
            for kind, way in ((1, 1), (3, 1), (4, 0), (5, 0), (6, 0), (6, 1), (7, 0), (7, 1)):
                got(half, kind, way)
        yield

    def block_at(d):
        return zl + sum(bit - 2 * bit * (zl // bit % 2) for bit in (8, 4, 2, 1) if d & bit)

    far_dev = {8: dev_far_8, 4: dev_far_4, 2: dev_far_2, 1: dev_far_1}
    w_copies = {}

    def hand_on(d):
        ref = wbuf.at[core, block_at(d)]
        if d:
            w_copies[d].wait_recv()
        for bit in (8, 4, 2, 1):
            if d & (2 * bit - 1) == 0:
                copy = remote(ref, ref, w_send.at[d + bit], w_recv.at[d + bit], far_dev[bit])
                copy.start()
                pending.append(copy)
                w_copies[d + bit] = copy

    def swap_rows():
        for d in range(1, 16, 2):
            w_copies[d].wait_recv()
        copy = remote(wbuf.at[core], wbuf.at[core], w_send.at[0], w_recv.at[0], {"core": 1 - core})
        copy.start()
        pending.append(copy)
        return copy

    def slab_copy(which, peer):
        return remote(
            sbuf.at[which, peer],
            rbuf.at[which, me],
            a_send.at[which, peer],
            a_recv.at[which, me],
            {"zl": peer // 2, "core": peer % 2},
        )

    def all_to_all_start(which):
        mine = pltpu.make_async_copy(sbuf.at[which, me], rbuf.at[which, me], a_recv.at[which, me])
        mine.start()

        def body(d, carry):
            slab_copy(which, (me + d) % 32).start()
            return carry

        lax.fori_loop(1, 32, body, 0)

    def all_to_all_wait(which):
        def body(d, carry):
            src = (me + d) % 32
            remote(
                sbuf.at[which, src], rbuf.at[which, src], a_send.at[which, src], a_recv.at[which, src],
                {"zl": src // 2, "core": src % 2},
            ).wait_recv()
            return carry

        lax.fori_loop(1, 32, body, 0)
        pltpu.make_async_copy(sbuf.at[which, me], rbuf.at[which, me], a_recv.at[which, me]).wait()

    def all_to_all_sent(which):
        def body(d, carry):
            slab_copy(which, (me + d) % 32).wait_send()
            return carry

        lax.fori_loop(1, 32, body, 0)

    def to_slabs(which, values):
        for p in range(4):
            rows[pl.ds(p, 128, stride=4), :] = values[p * 128 : p * 128 + 128, :].T
        sbuf[which] = rows[...].astype(BF).reshape(32, 16, 128)

    def from_slabs(which, out):
        rows[...] = rbuf[which].astype(F32).reshape(512, 128)
        for p in range(4):
            out[p * 128 : p * 128 + 128, :] = rows[pl.ds(p, 128, stride=4), :].T.astype(BF)

    def signals(which):
        rows[...] = rbuf[which].astype(F32).reshape(512, 128)
        return [
            jnp.concatenate([rows[pl.ds(ch * 4 + p, 32, stride=16), :] for p in range(4)], axis=0)
            for ch in range(4)
        ]

    def back_slabs(which, result):
        for ch in range(4):
            for p in range(4):
                rows[pl.ds(ch * 4 + p, 32, stride=16), :] = result[
                    p * 32 : p * 32 + 32, ch * 128 : ch * 128 + 128
                ]
        sbuf[which] = rows[...].astype(BF).reshape(32, 16, 128)

    def tables():
        return (
            (f1h[...], f1l[...]),
            (tre[...], tim[...]),
            (s2h[...], s2l[...]),
            (b2h[...], b2l[...]),
            (i1h[...], i1l[...]),
        )

    def multiply(slot):
        total = None
        for yy in range(4):
            for xx in range(4):
                part = lax.dot_general(
                    gbuf[slot, yy, xx],
                    wbuf[slot, yy * 4 + xx],
                    (((1,), (1,)), ((), ())),
                    preferred_element_type=F32,
                )
                total = part if total is None else total + part
        return total

    own_w.wait()
    hand_on(0)
    own_g.wait()
    own = plane(zh, 0)
    next(own)
    loads[0].wait()
    loads[1].wait()
    gated = (k[...].astype(F32) * v[...].astype(F32)).astype(BF).astype(F32)
    to_slabs(0, gated)
    next(own)
    next(own)
    next(own)
    on_up, on_dn = second_legs()
    next(own)
    next(own)
    hand_on(2)
    hand_on(4)
    hand_on(6)
    hand_on(8)
    for load in loads[2:]:
        load.wait()
    first, twist, second, second_back, first_back = tables()
    on_up.wait_recv()
    on_dn.wait_recv()
    rest = plane(other, 1)
    next(rest)
    next(rest)
    hand_on(10)
    hand_on(12)
    hand_on(14)
    next(rest)
    swap = swap_rows()
    swap.wait_recv()
    all_to_all_start(0)
    acc[...] = multiply(zh)
    for n in range(128):
        rows[n * 4 : n * 4 + 4, :] = f[:, n * 128 : n * 128 + 128]
    filters = [
        jnp.concatenate([rows[pl.ds(p * 4 + ch, 32, stride=16), :] for p in range(4)], axis=0)
        for ch in range(4)
    ]
    fspec[...] = forward(filters, first, twist, second, False)
    next(rest)
    next(rest)
    next(rest)
    mixed = (acc[...] + multiply(other)).astype(BF)
    gm_o[...] = mixed
    to_slabs(1, mixed.astype(F32) * q[...].astype(F32))
    all_to_all_start(1)
    all_to_all_wait(0)
    gspec[...] = forward(signals(0), first, twist, second, True)
    f_re, f_im = (fspec[:, 0:128], fspec[:, 128:256])
    g_re, g_im = (gspec[:, 0:128], gspec[:, 128:256])
    back_slabs(
        2, backward(f_re * g_re - f_im * g_im, f_re * g_im + f_im * g_re, first_back, twist, second_back)
    )
    all_to_all_start(2)
    all_to_all_wait(1)
    spec = forward(signals(1), first, twist, second, True)
    s_re, s_im = (spec[:, 0:128], spec[:, 128:256])
    f_re, f_im = (fspec[:, 0:128], fspec[:, 128:256])
    back_slabs(
        3, backward(s_re * f_re + s_im * f_im, s_im * f_re - s_re * f_im, first_back, twist, second_back)
    )
    all_to_all_start(3)
    g_re, g_im = (gspec[:, 0:128], gspec[:, 128:256])
    lags = backward(s_re * g_re + s_im * g_im, s_im * g_re - s_re * g_im, first_back, twist, second_back)
    for ch in range(4):
        for p in range(4):
            fg_o[ch, pl.ds(p, 32, stride=4), :] = (
                lags[p * 32 : p * 32 + 32, ch * 128 : ch * 128 + 128] * (1.0 / 128.0)
            )
    outs = [
        pltpu.make_async_copy(src, dst, out_sem.at[i])
        for i, (src, dst) in enumerate(((gm_o, gm_h), (fg_o, fg_h), (conv_o, conv_h)))
    ]
    outs[0].start()
    outs[1].start()
    all_to_all_wait(2)
    from_slabs(2, conv_o)
    outs[2].start()
    all_to_all_wait(3)
    from_slabs(3, gg_o)
    for out in outs:
        out.wait()

    for copy in pending:
        copy.wait_send()
    for which in range(4):
        all_to_all_sent(which)


def product(left, right):
    return (left.astype(F32) * right.astype(F32)).astype(BF)


def body(grad_out, proj_out, query, key_in, value_in, filters):
    tables = make_tables()
    operands = (grad_out, proj_out, query, key_in, value_in, filters, *tables)
    tile = jax.ShapeDtypeStruct((512, 128), BF)
    vmem = pl.BlockSpec(memory_space=pltpu.VMEM)
    far = pl.BlockSpec(memory_space=pl.ANY)
    dma = pltpu.SemaphoreType.DMA
    mixed, conv_out, grad_gated, filter_grad = pl.pallas_call(
        kernel,
        out_shape=(tile, tile, tile, jax.ShapeDtypeStruct((4, 128, 128), F32)),
        in_specs=[far] * len(operands),
        out_specs=(far, far, vmem, far),
        scratch_shapes=[
            pltpu.VMEM((2, 4, 4, 512, 128), BF),
            pltpu.VMEM((2, 16, 128, 128), BF),
            pltpu.VMEM((2, 256, 128), BF),
            pltpu.VMEM((4, 32, 16, 128), BF),
            pltpu.VMEM((4, 32, 16, 128), BF),
            pltpu.VMEM((512, 128), F32),
            pltpu.VMEM((512, 128), F32),
            pltpu.VMEM((512, 256), F32),
            pltpu.VMEM((512, 256), F32),
            *(pltpu.VMEM(operand.shape, operand.dtype) for operand in operands[2:]),
            dma((2,)),
            dma((14,)),
            dma((4,)),
            dma((4,)),
            dma((2, 2, 8, 2)),
            dma((2, 2, 8, 2)),
            dma((16,)),
            dma((16,)),
            dma((4, 32)),
            dma((4, 32)),
            pltpu.VMEM((512, 128), BF),
            pltpu.VMEM((512, 128), BF),
            pltpu.VMEM((4, 128, 128), F32),
            dma((3,)),
        ],
        compiler_params=pltpu.CompilerParams(collective_id=0, has_side_effects=True),
        name="mixer_backward",
    )(*operands)
    grad_query = product(mixed, conv_out)
    grad_key = product(grad_gated, value_in)
    grad_value = product(grad_gated, key_in)
    return (grad_query, grad_key, grad_value, filter_grad.reshape(4, 16384))


def solution(mesh):
    finer = Mesh(mesh.devices.reshape(16, 2, 4, 4, 2), CTX + MP)
    in_specs = (P(CTX, MP), P(MP, CTX), P(CTX, MP), P(CTX, MP), P(CTX, MP), P(EVERY, None))
    out_specs = (P(CTX, MP), P(CTX, MP), P(CTX, MP), P(EVERY, None))
    return jax.shard_map(body, mesh=finer, in_specs=in_specs, out_specs=out_specs, check_vma=False)
```
